256 devices in a mesh: gx: 64 (over y, z, core), gy: 4 (over x).
Axes of the slice: x: 4, y: 4, z: 8, core: 2. Of those that a mesh axis runs over, the one named last changes fastest.
Arguments:
- rhs: float32 [512, 256, 256], P('gx', 'gy'), may hold values from -12 to 12
- coefs: float32 [13, 512, 256, 256], P(None, 'gx', 'gy'), may hold values from 0 to 1.4, as said below
- shifts: float32 [4], replicated, may hold values from 0.4 to 1.1
Outputs:
- basis: float32 [5, 512, 256, 256], P(None, 'gx', 'gy')
- factor: float32 [5, 5], replicated
- solution: float32 [512, 256, 256], P('gx', 'gy')
- residual: float32 [512, 256, 256], P('gx', 'gy')
The draws below stay inside these ranges and needn't reach their ends.
Inputs may be any that keep to these rules, and one draw needn't show every extreme that they name: `coefs`: entry 0 lies in 0.6 to 1.4, entries 1 to 6 in 0.02 to 0.22, entries 7 to 12 in 0 to 0.16.
All inputs are finite; a program needn't handle non-finite values.
Results may differ from the reference program's by a relative error of at most 0.00095.
Values sent between devices are 32-bit elements; how exact they have to be, the bound alone decides.
No kernel may reach another device: no remote copies, remote signals or barrier semaphores. Data moves between devices by JAX's collectives and lax.ppermute only.
A program may use at most 64 MiB of HBM per device.

```python
import jax
import jax.numpy as jnp
from jax import lax

NZ = 256
STEPS = 4
NX = 512
NY = 256


def draw_rhs(key, part):
    noise_key, scale_key = jax.random.split(jax.random.fold_in(key, 11))
    scales = jnp.exp(jax.random.uniform(scale_key, (NX, NY, NZ), jnp.float32, jnp.log(0.1), 0.0))
    plane = jnp.arange(NX, dtype=jnp.float32)
    rising = (1.0 + 2.0 * plane / max(NX - 1, 1))[:, None, None]
    noise = jax.random.truncated_normal(noise_key, -4.0, 4.0, (NX, NY, NZ), jnp.float32)
    return noise * scales * rising


def draw_coefs(key, part):
    lower = jnp.array([0.6] + [0.02] * 6 + [0.0] * 6, jnp.float32)[:, None, None, None]
    upper = jnp.array([1.4] + [0.22] * 6 + [0.16] * 6, jnp.float32)[:, None, None, None]
    unit = jax.random.uniform(jax.random.fold_in(key, 23), (13, NX, NY, NZ), jnp.float32)
    return lower + (upper - lower) * unit


def setup_inputs(seed: int = 0) -> dict:
    splits = jax.random.split(jax.random.key(seed), 4)
    rhs = draw_rhs(jax.random.fold_in(splits[3], 71), 0)
    coefs = draw_coefs(jax.random.fold_in(splits[3], 71), 0)
    shifts = jnp.clip(jax.random.uniform(splits[2], (STEPS,), jnp.float32, 0.4, 1.1), 0.4, 1.1)
    return {"rhs": rhs, "coefs": coefs, "shifts": shifts}


growth = 2.0

def neighbours(field):
    minus_x = jnp.roll(field, 1, axis=0)
    plus_x = jnp.roll(field, -1, axis=0)
    padded = jnp.pad(field, ((0, 0), (1, 1), (1, 1)))
    minus_y = padded[:, :-2, 1:-1]
    plus_y = padded[:, 2:, 1:-1]
    minus_z = padded[:, 1:-1, :-2]
    plus_z = padded[:, 1:-1, 2:]
    return (minus_x, plus_x, minus_y, plus_y, minus_z, plus_z)

def apply_spai(field, coefs):
    total = coefs[0] * field
    near = neighbours(field)
    for index in range(6):
        total = total + coefs[1 + index] * near[index]
    return total

def apply_operator(field, coefs):
    total = field
    near = neighbours(field)
    for index in range(6):
        total = total - coefs[7 + index] * near[index]
    return total

def invert_upper(upper):
    order = upper.shape[0]
    identity = jnp.eye(order, dtype=upper.dtype)
    result = jnp.zeros_like(upper)
    for row in range(order - 1, -1, -1):
        known = identity[row] - jnp.dot(upper[row], result, precision=lax.Precision.HIGHEST)
        result = result.at[row].set(known / upper[row, row])
    return result

def least_squares(factor, shifts):
    count = shifts.shape[0]
    relation = jnp.zeros((count + 1, count), jnp.float32)
    for column in range(count):
        relation = relation.at[column, column].set(shifts[column])
        relation = relation.at[column + 1, column].set(1.0 / growth)
    hessenberg = jnp.dot(factor, relation, precision=lax.Precision.HIGHEST)
    target = factor[:, 0]
    for column in range(count):
        top = hessenberg[column]
        below = hessenberg[column + 1]
        radius = jnp.sqrt(top[column] ** 2 + below[column] ** 2)
        cosine = top[column] / radius
        sine = below[column] / radius
        hessenberg = hessenberg.at[column].set(cosine * top + sine * below)
        hessenberg = hessenberg.at[column + 1].set(cosine * below - sine * top)
        first_entry = target[column]
        second_entry = target[column + 1]
        target = target.at[column].set(cosine * first_entry + sine * second_entry)
        target = target.at[column + 1].set(cosine * second_entry - sine * first_entry)
    upper = hessenberg[:count]
    weights = jnp.dot(invert_upper(upper), target[:count], precision=lax.Precision.HIGHEST)
    combine = -jnp.dot(relation, weights, precision=lax.Precision.HIGHEST)
    combine = combine.at[0].add(1.0)
    return (weights, combine)

def reference(rhs, coefs, shifts):
    count = shifts.shape[0]
    basis_list = [rhs]
    images = []
    for step in range(count):
        image = apply_spai(basis_list[step], coefs)
        images.append(image)
        applied = apply_operator(image, coefs)
        basis_list.append(growth * (applied - shifts[step] * basis_list[step]))
    stacked = jnp.stack(basis_list)
    flat = stacked.reshape(count + 1, -1)
    gram = jnp.dot(flat, flat.T, precision=lax.Precision.HIGHEST) / flat.shape[1]
    factor = jnp.linalg.cholesky(gram).T
    inverse = invert_upper(factor)
    ortho = jnp.dot(inverse.T, flat, precision=lax.Precision.HIGHEST).reshape(stacked.shape)
    weights, combine = least_squares(factor, shifts)
    image_flat = jnp.stack(images).reshape(count, -1)
    solution = jnp.dot(weights, image_flat, precision=lax.Precision.HIGHEST).reshape(rhs.shape)
    residual = jnp.dot(combine, flat, precision=lax.Precision.HIGHEST).reshape(rhs.shape)
    return (ortho, factor, solution, residual)
```

```python
import jax
import jax.numpy as jnp
from jax import lax
from jax.experimental import pallas as pl
from jax.experimental.pallas import tpu as pltpu
from jax.sharding import Mesh
from jax.sharding import PartitionSpec as P

GX = ("gx_0", "gx_1", "gx_2")
EVERY = ("gx_0", "gx_1", "gx_2", "gy")
F32 = jnp.float32
GROWTH = 2.0
LIMIT = 48 * 1024 * 1024

VM = pl.BlockSpec(memory_space=pltpu.VMEM)
SM = pl.BlockSpec(memory_space=pltpu.SMEM)
ANY = pl.BlockSpec(memory_space=pl.ANY)


def on_chip(*shape):
    return pltpu.VMEM(shape, F32)


def pinned(array):
    return pltpu.with_memory_space_constraint(array, pltpu.VMEM)


def call(kernel, name, ins, specs, outs, out_specs=None, scratch=()):
    ins = [pinned(a) if s is VM else a for a, s in zip(ins, specs)]
    return pl.pallas_call(
        kernel,
        name=name,
        out_shape=outs,
        in_specs=specs,
        out_specs=out_specs if out_specs is not None else [VM] * len(outs),
        scratch_shapes=scratch,
        compiler_params=pltpu.CompilerParams(vmem_limit_bytes=LIMIT),
    )(*ins)


def shifted(plane, above, below):
    rows, lanes = plane.shape
    row = lax.broadcasted_iota(jnp.int32, plane.shape, 0)
    lane = lax.broadcasted_iota(jnp.int32, plane.shape, 1)
    minus_y = jnp.where(row == 0, above, pltpu.roll(plane, 1, 0))
    plus_y = jnp.where(row == rows - 1, below, pltpu.roll(plane, rows - 1, 0))
    minus_z = jnp.where(lane == 0, 0.0, pltpu.roll(plane, 1, 1))
    plus_z = jnp.where(lane == lanes - 1, 0.0, pltpu.roll(plane, lanes - 1, 1))
    return minus_y, plus_y, minus_z, plus_z


def neighbours(field, p, halo, edge):
    minus_x, plus_x, above, below = halo
    planes = field.shape[0]
    centre = field[p]
    before = minus_x[...] if p == 0 else field[p - 1]
    after = plus_x[...] if p == planes - 1 else field[p + 1]
    up = above[p : p + 1, :] * edge[0]
    down = below[p : p + 1, :] * edge[1]
    return centre, (before, after) + shifted(centre, up, down)


def put_edges(p, value, planes, x_low, x_high, y_low, y_high):
    rows = value.shape[0]
    if p == 0:
        x_low[...] = value
    if p == planes - 1:
        x_high[...] = value
    y_low[p : p + 1, :] = value[:1]
    y_high[p : p + 1, :] = value[rows - 1 :]


def load_kernel(coefs, wide, sems):
    copies = [pltpu.make_async_copy(coefs.at[i], wide.at[i], sems.at[i]) for i in range(coefs.shape[0])]
    for copy in copies:
        copy.start()
    for copy in copies:
        copy.wait()


def edge_kernel(rhs, x_low, x_high, y_low, y_high):
    planes = rhs.shape[0]
    for p in range(planes):
        put_edges(p, rhs[p], planes, x_low, x_high, y_low, y_high)


def spai_kernel(edge, coefs, v, mx, px, my, py, w, x_low, x_high, y_low, y_high):
    planes = v.shape[0]
    for p in range(planes):
        centre, near = neighbours(v, p, (mx, px, my, py), edge)
        total = coefs[0, p] * centre
        for d in range(6):
            total = total + coefs[1 + d, p] * near[d]
        w[p] = total
        put_edges(p, total, planes, x_low, x_high, y_low, y_high)


def apply_kernel(edge, coefs, shift, v, w, mx, px, my, py, out, x_low, x_high, y_low, y_high):
    planes = v.shape[0]
    for p in range(planes):
        centre, near = neighbours(w, p, (mx, px, my, py), edge)
        total = centre
        for d in range(6):
            total = total - coefs[7 + d, p] * near[d]
        total = GROWTH * (total - shift[0] * v[p])
        out[p] = total
        put_edges(p, total, planes, x_low, x_high, y_low, y_high)


def pair_rows(count):
    return [(i, j) for j in range(count) for i in range(j + 1)]


def gram_accumulate(lefts, right, rows):
    planes = right.shape[0]
    sums = [jnp.zeros((8, 256), F32) for _ in lefts]
    for p in range(planes):
        for r in range(0, right.shape[1], 8):
            value = right[p, r : r + 8, :]
            for k, left in enumerate(lefts):
                other = value if left is right else left[p, r : r + 8, :]
                sums[k] = sums[k] + other * value
    return [jnp.sum(s[:, :128] + s[:, 128:], axis=0, keepdims=True) for s in sums]


def early_gram_kernel(v0, v1, v2, v3, out):
    fields = (v0, v1, v2, v3)
    k = 0
    out[...] = jnp.zeros_like(out)
    for j in range(4):
        for part in gram_accumulate(fields[: j + 1], fields[j], None):
            out[k : k + 1, :] = part
            k += 1


def late_gram_kernel(early, v0, v1, v2, v3, v4, out, hold):
    fields = (v0, v1, v2, v3, v4)
    hold[...] = early[...]
    for k, part in enumerate(gram_accumulate(fields, v4, None)):
        hold[10 + k : 11 + k, :] = part
    totals = jnp.sum(hold[...], axis=1, keepdims=True)
    row = lax.broadcasted_iota(jnp.int32, (16, 128), 0)
    lane = lax.broadcasted_iota(jnp.int32, (16, 128), 1)
    line = jnp.sum(jnp.where(row == lane, totals, 0.0), axis=0, keepdims=True)
    out[...] = jnp.broadcast_to(line, out.shape)


def solve(gram, shifts):
    n = 5
    zero = jnp.zeros_like(gram[0][0])
    one = jnp.ones_like(zero)
    lower = [[zero] * n for _ in range(n)]
    for j in range(n):
        rest = gram[j][j]
        for k in range(j):
            rest = rest - lower[j][k] * lower[j][k]
        pivot = jnp.sqrt(rest)
        lower[j][j] = pivot
        for i in range(j + 1, n):
            rest = gram[i][j]
            for k in range(j):
                rest = rest - lower[i][k] * lower[j][k]
            lower[i][j] = rest / pivot
    factor = [[lower[j][i] for j in range(n)] for i in range(n)]

    def invert(upper, order):
        result = [[zero] * order for _ in range(order)]
        for row in range(order - 1, -1, -1):
            for column in range(row, order):
                known = one if column == row else zero
                for k in range(row + 1, column + 1):
                    known = known - upper[row][k] * result[k][column]
                result[row][column] = known / upper[row][row]
        return result

    inverse = invert(factor, n)
    count = n - 1
    hess = [[None] * count for _ in range(n)]
    for row in range(n):
        for column in range(count):
            entry = zero
            if column >= row:
                entry = entry + factor[row][column] * shifts[column]
            if column + 1 >= row:
                entry = entry + factor[row][column + 1] * (1.0 / GROWTH)
            hess[row][column] = entry
    target = [factor[0][0]] + [zero] * (n - 1)
    for column in range(count):
        top, below = hess[column], hess[column + 1]
        radius = jnp.sqrt(top[column] * top[column] + below[column] * below[column])
        cosine = top[column] / radius
        sine = below[column] / radius
        hess[column] = [cosine * t + sine * b for t, b in zip(top, below)]
        hess[column + 1] = [cosine * b - sine * t for t, b in zip(top, below)]
        first, second = target[column], target[column + 1]
        target[column] = cosine * first + sine * second
        target[column + 1] = cosine * second - sine * first
    upper_inverse = invert(hess, count)
    weights = []
    for row in range(count):
        entry = zero
        for k in range(row, count):
            entry = entry + upper_inverse[row][k] * target[k]
        weights.append(entry)
    combine = []
    for row in range(n):
        entry = one if row == 0 else zero
        if row < count:
            entry = entry - shifts[row] * weights[row]
        if row > 0:
            entry = entry - (1.0 / GROWTH) * weights[row - 1]
        combine.append(entry)
    return factor, inverse, weights, combine


def final_kernel(cells, shifts, rows, v0, v1, v2, v3, v4, w0, w1, w2, w3,
                 basis, factor_out, solution_out, residual_out, made, sems):
    line = jnp.sum(rows[...], axis=0, keepdims=True) * (1.0 / cells)
    gram = [[None] * 5 for _ in range(5)]
    for k, (i, j) in enumerate(pair_rows(5)):
        entry = jnp.broadcast_to(line[:, k : k + 1], (8, 128))
        gram[i][j] = entry
        gram[j][i] = entry
    factor, inverse, weights, combine = solve(gram, [shifts[k] for k in range(4)])
    row = lax.broadcasted_iota(jnp.int32, (8, 128), 0)
    lane = lax.broadcasted_iota(jnp.int32, (8, 128), 1)
    table = jnp.zeros((8, 128), F32)
    for i in range(5):
        for j in range(i, 5):
            table = jnp.where((row == i) & (lane == j), factor[i][j], table)
    factor_out[...] = table[:5, :5]
    fields = (v0, v1, v2, v3, v4)
    images = (w0, w1, w2, w3)
    planes = v0.shape[0]
    copies = []
    for p in range(planes):
        for r in range(0, v0.shape[1], 8):
            for c in range(0, v0.shape[2], 128):
                v = [f[p, r : r + 8, c : c + 128] for f in fields]
                w = [f[p, r : r + 8, c : c + 128] for f in images]
                for k in range(5):
                    total = inverse[0][k] * v[0]
                    for j in range(1, k + 1):
                        total = total + inverse[j][k] * v[j]
                    made[k, p, r : r + 8, c : c + 128] = total
                total = weights[0] * w[0]
                for k in range(1, 4):
                    total = total + weights[k] * w[k]
                made[5, p, r : r + 8, c : c + 128] = total
                total = combine[0] * v[0]
                for j in range(1, 5):
                    total = total + combine[j] * v[j]
                made[6, p, r : r + 8, c : c + 128] = total
        for n, (source, target) in enumerate(
            ((made.at[0:5, p], basis.at[:, p]), (made.at[5, p], solution_out.at[p]), (made.at[6, p], residual_out.at[p]))
        ):
            copy = pltpu.make_async_copy(source, target, sems.at[p, n])
            copy.start()
            copies.append(copy)
    for copy in copies:
        copy.wait()


def ring(count, step):
    return [(i, (i + step) % count) for i in range(count)]


def exchange(edges):
    x_low, x_high, y_low, y_high = edges
    nx, ny = lax.axis_size(GX), lax.axis_size("gy")
    return (
        lax.ppermute(x_high, GX, ring(nx, 1)),
        lax.ppermute(x_low, GX, ring(nx, -1)),
        lax.ppermute(y_high, "gy", ring(ny, 1)),
        lax.ppermute(y_low, "gy", ring(ny, -1)),
    )


def body(rhs, coefs, shifts):
    planes, rows, lanes = rhs.shape
    field = on_chip(planes, rows, lanes)
    edges = [on_chip(rows, lanes), on_chip(rows, lanes), on_chip(planes, lanes), on_chip(planes, lanes)]
    place = lax.axis_index("gy")
    last = lax.axis_size("gy") - 1
    edge = jnp.stack([(place > 0).astype(F32), (place < last).astype(F32)])
    (near,) = call(
        load_kernel, "load", [coefs], [ANY], [on_chip(*coefs.shape)],
        scratch=[pltpu.SemaphoreType.DMA((coefs.shape[0],))],
    )
    halo = exchange(call(edge_kernel, "edges", [rhs], [VM], edges))
    basis, images = [rhs], []
    for step in range(4):
        w, *cut = call(spai_kernel, "spai", [edge, near, basis[step], *halo], [SM] + [VM] * 6, [field] + edges)
        images.append(w)
        halo = exchange(cut)
        v, *cut = call(
            apply_kernel, "apply", [edge, near, shifts[step : step + 1], basis[step], w, *halo],
            [SM, VM, SM] + [VM] * 6, [field] + edges,
        )
        basis.append(v)
        if step < 3:
            halo = exchange(cut)
    (early,) = call(early_gram_kernel, "early_gram", basis[:4], [VM] * 4, [on_chip(16, 128)])
    devices = lax.axis_size(GX) * lax.axis_size("gy")
    (line,) = call(
        late_gram_kernel, "late_gram", [early, *basis], [VM] * 6, [on_chip(devices, 128)],
        scratch=[pltpu.VMEM((16, 128), F32)],
    )
    lines = lax.all_to_all(line, EVERY, 0, 0, tiled=True)
    cells = float(planes * rows * lanes * devices)
    whole = jax.ShapeDtypeStruct((planes, rows, lanes), F32)
    return tuple(
        call(
            lambda *refs: final_kernel(cells, *refs), "final",
            [shifts, lines, *basis, *images], [SM] + [VM] * 10,
            [jax.ShapeDtypeStruct((5, planes, rows, lanes), F32), jax.ShapeDtypeStruct((5, 5), F32), whole, whole],
            out_specs=[ANY, VM, ANY, ANY],
            scratch=[pltpu.VMEM((7, planes, rows, lanes), F32), pltpu.SemaphoreType.DMA((planes, 3))],
        )
    )


def solution(mesh):
    torus = Mesh(mesh.devices.reshape(4, 8, 2, mesh.shape["gy"]), EVERY)
    in_specs = (P(GX, "gy", None), P(None, GX, "gy", None), P())
    out_specs = (P(None, GX, "gy", None), P(), P(GX, "gy", None), P(GX, "gy", None))
    return jax.shard_map(body, mesh=torus, in_specs=in_specs, out_specs=out_specs, check_vma=False)
```

```python
import functools

import jax
import jax.numpy as jnp
from jax import lax
from jax.experimental import pallas as pl
from jax.experimental.pallas import tpu as pltpu
from jax.sharding import Mesh
from jax.sharding import PartitionSpec as P

GX = ("gx_0", "gx_1", "gx_2")
EVERY = ("gx_0", "gx_1", "gx_2", "gy")
F32 = jnp.float32
GROWTH = 2.0
LIMIT = 8 * 1024 * 1024

VM = pl.BlockSpec(memory_space=pltpu.VMEM)
SM = pl.BlockSpec(memory_space=pltpu.SMEM)
ANY = pl.BlockSpec(memory_space=pl.ANY)


def on_chip(*shape):
    return pltpu.VMEM(shape, F32)


def pinned(array):
    return pltpu.with_memory_space_constraint(array, pltpu.VMEM)


def in_hbm(array):
    return pltpu.with_memory_space_constraint(array, pltpu.HBM)


def call(kernel, name, ins, specs, outs, out_specs=None, scratch=(), aliases=None):
    ins = [pinned(a) if s is VM else in_hbm(a) if s is ANY else a for a, s in zip(ins, specs)]
    return pl.pallas_call(
        kernel,
        name=name,
        out_shape=outs,
        in_specs=specs,
        out_specs=out_specs if out_specs is not None else [VM] * len(outs),
        scratch_shapes=scratch,
        input_output_aliases=aliases or {},
        compiler_params=pltpu.CompilerParams(vmem_limit_bytes=LIMIT),
    )(*ins)


G = 8


def run_copies(pairs, sems):
    copies = [pltpu.make_async_copy(s, t, sems.at[n]) for n, (s, t) in enumerate(pairs)]
    for copy in copies:
        copy.start()
    for copy in copies:
        copy.wait()


def cut_kernel(rhs, coefs, x_low, x_high, y_low, y_high, sems):
    planes, rows = rhs.shape[0], rhs.shape[1]
    pairs = [
        (rhs.at[0:2], x_low.at[0:2]),
        (coefs.at[0:7, 0], x_low.at[2:9]),
        (rhs.at[planes - 2 : planes], x_high.at[0:2]),
        (coefs.at[0:7, planes - 1], x_high.at[2:9]),
    ]
    for y, span in ((y_low, slice(0, G)), (y_high, slice(rows - G, rows))):
        for p in range(planes):
            pairs.append((rhs.at[p, span], y.at[0, G * p : G * p + G]))
            pairs.append((coefs.at[:, p, span], y.at[1:14, G * p : G * p + G]))
    run_copies(pairs, sems)


def load_kernel(rhs, coefs, after, field, own, sems):
    planes, rows = rhs.shape[0], rhs.shape[1]
    pairs = [(rhs, field.at[2 : planes + 2, G : rows + G])]
    for p in range(planes):
        pairs.append((coefs.at[:, p], own.at[:, rows * p : rows * p + rows]))
    run_copies(pairs, sems)


def relay_kernel(x_below, x_above, after, y_low, y_high):
    rows = x_below.shape[1]
    for n, x in enumerate((x_below, x_above)):
        y_low[n] = x[:, 0:G]
        y_high[n] = x[:, rows - G : rows]


def tile_at(row):
    return pl.ds(pl.multiple_of(row, 8), 8)


class Coefficients:
    def __init__(self, rows, own, y_below, y_above, corners=None):
        self.own, self.y_below, self.y_above, self.corners = own, y_below, y_above, corners
        self.rows, self.tiles = rows, rows // 8 + 2

    def spai(self, d, q, t):
        return self.plane(d, q, t)

    def oper(self, d, p, t):
        return self.plane(7 + d, p, t)

    def plane(self, d, p, t):
        if t == 0:
            return self.y_below[1 + d, tile_at(G * p), :]
        if t == self.tiles - 1:
            return self.y_above[1 + d, tile_at(G * p), :]
        return self.own[d, tile_at(self.rows * p + 8 * t - 8), :]

    def ghost(self, d, side, t):
        x, c_below, c_above = self.corners[side]
        if t == 0:
            return c_below[side, 2 + d]
        if t == self.tiles - 1:
            return c_above[side, 2 + d]
        return x[2 + d, 8 * t - 8 : 8 * t, :]


def edges():
    place = lax.axis_index("gy")
    last = lax.axis_size("gy") - 1
    return jnp.where(place > 0, 1.0, 0.0), jnp.where(place < last, 1.0, 0.0)


def within(edge, t, tiles, value):
    if t == 0:
        return value * edge[0]
    if t == tiles - 1:
        return value * edge[1]
    return value


def stencil(field, at, emit):
    tiles = field.shape[1] // 8
    lanes = field.shape[2]
    row = lax.broadcasted_iota(jnp.int32, (8, lanes), 0)
    lane = lax.broadcasted_iota(jnp.int32, (8, lanes), 1)
    top, bottom = row == 0, row == 7
    left, right = lane == 0, lane == lanes - 1

    def tile(t):
        value = field[at, 8 * t : 8 * t + 8, :]
        return value, pltpu.roll(value, 1, 0), pltpu.roll(value, 7, 0)

    before = here = tile(0)
    for t in range(tiles):
        after = tile(t + 1) if t + 1 < tiles else here
        value = here[0]
        span = slice(8 * t, 8 * t + 8)
        near = (
            field[at - 1, span, :],
            field[at + 1, span, :],
            jnp.where(top, before[1], here[1]),
            jnp.where(bottom, after[2], here[2]),
            jnp.where(left, 0.0, pltpu.roll(value, 1, 1)),
            jnp.where(right, 0.0, pltpu.roll(value, lanes - 1, 1)),
        )
        emit(t, span, value, near)
        before, here = here, after


def spai_plane(edge, coefficient, field, image, q):
    def emit(t, span, value, near):
        total = coefficient(0, t) * value
        for d in range(6):
            total = total + coefficient(1 + d, t) * near[d]
        image[q + 1, span, :] = within(edge, t, image.shape[1] // 8, total)

    stencil(field, q + 2, emit)


def oper_plane(edge, shift, coefs, field, image, out, p):
    def emit(t, span, value, near):
        total = value - shift * field[p + 2, span, :]
        for d in range(6):
            total = total - coefs.oper(d, p, t) * near[d]
        out[p + 2, span, :] = within(edge, t, out.shape[1] // 8, GROWTH * total)

    stencil(image, p + 1, emit)


def each(first, count, jump, work):
    half = count // 2

    def one(n, carry):
        work(first + n + jump * (n // half))
        return carry

    lax.fori_loop(0, count, one, 0)


def inner_work(shift, edge, coefs, field, image, out):
    planes = image.shape[0] - 2
    each(1, planes - 2, 0, lambda q: spai_plane(edge, lambda d, t: coefs.spai(d, q, t), field, image, q))
    each(2, planes - 4, 0, lambda p: oper_plane(edge, shift, coefs, field, image, out, p))


def outer_work(shift, edge, coefs, field, image, out):
    planes = image.shape[0] - 2
    for side, q in enumerate((-1, planes)):
        spai_plane(edge, lambda d, t: coefs.ghost(d, side, t), field, image, q)
    each(0, 2, planes - 2, lambda q: spai_plane(edge, lambda d, t: coefs.spai(d, q, t), field, image, q))
    each(0, 4, planes - 4, lambda p: oper_plane(edge, shift, coefs, field, image, out, p))


def send_edges(out, x_low, x_high):
    planes = out.shape[0] - 4
    x_low[...] = out[2:4]
    x_high[...] = out[planes : planes + 2]


def first_inner_kernel(shifts, own, y_below, y_above, field0, field, image, out):
    edge = edges()
    planes, tall = image.shape[0] - 2, image.shape[1]
    for p in range(planes):
        field[p + 2, 0:G, :] = y_below[0, G * p : G * p + G, :] * edge[0]
        field[p + 2, tall - G : tall, :] = y_above[0, G * p : G * p + G, :] * edge[1]
    inner_work(shifts[0], edge, Coefficients(field.shape[1] - 2 * G, own, y_below, y_above), field, image, out)


def inner_kernel(step, shifts, own, y_below, y_above, field, image, out):
    inner_work(shifts[step], edges(), Coefficients(field.shape[1] - 2 * G, own, y_below, y_above), field, image, out)


def outer_kernel(step, shifts, own, y_below, y_above, x_below, x_above, c_below, c_above, *refs):
    edge = edges()
    first = step == 0
    if first:
        field0, image0, out0, field, image, out, *sends = refs
    else:
        if step == 3:
            refs = refs[1:]
        v_below, v_above, field0, image0, out0, field, image, out, *sends = refs
    planes, tall = image.shape[0] - 2, image.shape[1]
    if first:
        for side, (x, at) in enumerate(((x_below, 0), (x_above, planes + 2))):
            field[at : at + 2, 0:G, :] = c_below[side, 0:2] * edge[0]
            field[at : at + 2, G : tall - G, :] = x[0:2]
            field[at : at + 2, tall - G : tall, :] = c_above[side, 0:2] * edge[1]
    else:
        field[0:2] = v_below[...]
        field[planes + 2 : planes + 4] = v_above[...]
    corners = ((x_below, c_below, c_above), (x_above, c_below, c_above))
    outer_work(shifts[step], edge, Coefficients(field.shape[1] - 2 * G, own, y_below, y_above, corners), field, image, out)
    if sends:
        send_edges(out, *sends)


def pair_rows(count):
    return [(i, j) for j in range(count) for i in range(j + 1)]


def gram_rows(fields, pairs, out, start):
    planes = fields[0].shape[0] - 4
    rows = fields[0].shape[1] - 2 * G

    def one(p, sums):
        sums = list(sums)
        for r in range(G, rows + G, 8):
            values = [f[p + 2, r : r + 8, :] for f in fields]
            for k, (i, j) in enumerate(pairs):
                sums[k] = sums[k] + values[i] * values[j]
        return tuple(sums)

    zero = jnp.zeros((8, fields[0].shape[2]), F32)
    sums = lax.fori_loop(0, planes, one, tuple(zero for _ in pairs))
    for k, s in enumerate(sums):
        out[start + k : start + k + 1, :] = jnp.sum(s[:, :128] + s[:, 128:], axis=0, keepdims=True)


def early_gram_kernel(v0, v1, v2, v3, out):
    out[...] = jnp.zeros_like(out)
    gram_rows((v0, v1, v2, v3), pair_rows(4), out, 0)


def late_gram_kernel(early, v0, v1, v2, v3, v4, out, hold):
    hold[...] = early[...]
    gram_rows((v0, v1, v2, v3, v4), [(i, 4) for i in range(5)], hold, 10)
    totals = jnp.sum(hold[...], axis=1, keepdims=True)
    row = lax.broadcasted_iota(jnp.int32, (16, 128), 0)
    lane = lax.broadcasted_iota(jnp.int32, (16, 128), 1)
    line = jnp.sum(jnp.where(row == lane, totals, 0.0), axis=0, keepdims=True)
    out[...] = jnp.broadcast_to(line, out.shape)


def solve(gram, shifts):
    n = 5
    zero = jnp.zeros_like(gram[0][0])
    one = jnp.ones_like(zero)
    lower = [[zero] * n for _ in range(n)]
    for j in range(n):
        rest = gram[j][j]
        for k in range(j):
            rest = rest - lower[j][k] * lower[j][k]
        pivot = jnp.sqrt(rest)
        lower[j][j] = pivot
        for i in range(j + 1, n):
            rest = gram[i][j]
            for k in range(j):
                rest = rest - lower[i][k] * lower[j][k]
            lower[i][j] = rest / pivot
    factor = [[lower[j][i] for j in range(n)] for i in range(n)]

    def invert(upper, order):
        result = [[zero] * order for _ in range(order)]
        for row in range(order - 1, -1, -1):
            for column in range(row, order):
                known = one if column == row else zero
                for k in range(row + 1, column + 1):
                    known = known - upper[row][k] * result[k][column]
                result[row][column] = known / upper[row][row]
        return result

    inverse = invert(factor, n)
    count = n - 1
    hess = [[None] * count for _ in range(n)]
    for row in range(n):
        for column in range(count):
            entry = zero
            if column >= row:
                entry = entry + factor[row][column] * shifts[column]
            if column + 1 >= row:
                entry = entry + factor[row][column + 1] * (1.0 / GROWTH)
            hess[row][column] = entry
    target = [factor[0][0]] + [zero] * (n - 1)
    for column in range(count):
        top, below = hess[column], hess[column + 1]
        radius = jnp.sqrt(top[column] * top[column] + below[column] * below[column])
        cosine = top[column] / radius
        sine = below[column] / radius
        hess[column] = [cosine * t + sine * b for t, b in zip(top, below)]
        hess[column + 1] = [cosine * b - sine * t for t, b in zip(top, below)]
        first, second = target[column], target[column + 1]
        target[column] = cosine * first + sine * second
        target[column + 1] = cosine * second - sine * first
    upper_inverse = invert(hess, count)
    weights = []
    for row in range(count):
        entry = zero
        for k in range(row, count):
            entry = entry + upper_inverse[row][k] * target[k]
        weights.append(entry)
    combine = []
    for row in range(n):
        entry = one if row == 0 else zero
        if row < count:
            entry = entry - shifts[row] * weights[row]
        if row > 0:
            entry = entry - (1.0 / GROWTH) * weights[row - 1]
        combine.append(entry)
    return factor, inverse, weights, combine


def final_kernel(cells, shifts, rows, v0, v1, v2, v3, v4, w0, w1, w2, w3,
                 basis, factor_out, solution_out, residual_out, made, sems):
    line = jnp.sum(rows[...], axis=0, keepdims=True) * (1.0 / cells)
    gram = [[None] * 5 for _ in range(5)]
    for k, (i, j) in enumerate(pair_rows(5)):
        entry = jnp.broadcast_to(line[:, k : k + 1], (8, 128))
        gram[i][j] = entry
        gram[j][i] = entry
    factor, inverse, weights, combine = solve(gram, [shifts[k] for k in range(4)])
    row = lax.broadcasted_iota(jnp.int32, (8, 128), 0)
    lane = lax.broadcasted_iota(jnp.int32, (8, 128), 1)
    table = jnp.zeros((8, 128), F32)
    for i in range(5):
        for j in range(i, 5):
            table = jnp.where((row == i) & (lane == j), factor[i][j], table)
    factor_out[...] = table[:5, :5]
    fields = (v0, v1, v2, v3, v4)
    images = (w0, w1, w2, w3)
    planes = made.shape[1]

    def copies(p):
        triples = ((made.at[0:5, p], basis.at[:, p]), (made.at[5, p], solution_out.at[p]), (made.at[6, p], residual_out.at[p]))
        return [pltpu.make_async_copy(source, target, sems.at[p, n]) for n, (source, target) in enumerate(triples)]

    def one(p, carry):
        for r in range(0, made.shape[2], 8):
            for c in range(0, made.shape[3], 128):
                v = [f[p + 2, r + G : r + G + 8, c : c + 128] for f in fields]
                w = [f[p + 1, r + G : r + G + 8, c : c + 128] for f in images]
                for k in range(5):
                    total = inverse[0][k] * v[0]
                    for j in range(1, k + 1):
                        total = total + inverse[j][k] * v[j]
                    made[k, p, r : r + 8, c : c + 128] = total
                total = weights[0] * w[0]
                for k in range(1, 4):
                    total = total + weights[k] * w[k]
                made[5, p, r : r + 8, c : c + 128] = total
                total = combine[0] * v[0]
                for j in range(1, 5):
                    total = total + combine[j] * v[j]
                made[6, p, r : r + 8, c : c + 128] = total
        for copy in copies(p):
            copy.start()
        return carry

    def finish(p, carry):
        for copy in copies(p):
            copy.wait()
        return carry

    lax.fori_loop(0, planes, one, 0)
    lax.fori_loop(0, planes, finish, 0)


def ring(count, step):
    return [(i, (i + step) % count) for i in range(count)]


def both_ways(low, high, axis):
    count = lax.axis_size(axis)
    return lax.ppermute(high, axis, ring(count, 1)), lax.ppermute(low, axis, ring(count, -1))


def body(rhs, coefs, shifts):
    planes, rows, lanes = rhs.shape
    tall = rows + 2 * G
    field = on_chip(planes + 4, tall, lanes)
    image = on_chip(planes + 2, tall, lanes)
    halo = on_chip(2, tall, lanes)
    x_cut, y_cut = on_chip(9, rows, lanes), on_chip(14, G * planes, lanes)
    corner = on_chip(2, 9, G, lanes)
    x_low, x_high, y_low, y_high = call(
        cut_kernel, "cut", [rhs, coefs], [ANY] * 2, [x_cut, x_cut, y_cut, y_cut],
        scratch=[pltpu.SemaphoreType.DMA((4 + 4 * planes,))],
    )
    x_below, x_above = both_ways(x_low, x_high, GX)
    y_below, y_above = both_ways(y_low, y_high, "gy")
    v, own = call(
        load_kernel, "load", [rhs, coefs, y_low], [ANY, ANY, VM], [field, on_chip(13, planes * rows, lanes)],
        scratch=[pltpu.SemaphoreType.DMA((1 + planes,))],
    )
    c_low, c_high = call(relay_kernel, "relay", [x_below, x_above, own], [VM] * 3, [corner, corner])
    c_below, c_above = both_ways(c_low, c_high, "gy")
    basis, images = [], []
    for step in range(4):
        common = [shifts, own, y_below, y_above]
        specs = [SM] + [VM] * 3
        if step == 0:
            v, w, out = call(
                first_inner_kernel, "first_inner", common + [v], specs + [VM], [field, image, field], aliases={4: 0}
            )
        else:
            w, out = call(functools.partial(inner_kernel, step), "inner", common + [v], specs + [VM], [image, field])
        common += [x_below, x_above, c_below, c_above]
        if step == 3:
            (early,) = call(early_gram_kernel, "early_gram", basis + [v], [VM] * 4, [on_chip(16, 128)])
            common += [early]
        common += [] if step == 0 else [below, above]
        specs += [VM] * (len(common) - 4)
        at = len(common)
        v, w, out, *sends = call(
            functools.partial(outer_kernel, step),
            "first_outer" if step == 0 else "outer",
            common + [v, w, out], specs + [VM] * 3,
            [field, image, field] + [halo, halo] * (step < 3), aliases={at: 0, at + 1: 1, at + 2: 2},
        )
        if sends:
            below, above = both_ways(*sends, GX)
        basis.append(v)
        images.append(w)
        v = out
    basis.append(v)
    devices = lax.axis_size(GX) * lax.axis_size("gy")
    (line,) = call(
        late_gram_kernel, "late_gram", [early, *basis], [VM] * 6, [on_chip(devices, 128)],
        scratch=[pltpu.VMEM((16, 128), F32)],
    )
    lines = lax.all_to_all(line, EVERY, 0, 0, tiled=True)
    cells = float(planes * rows * lanes * devices)
    whole = jax.ShapeDtypeStruct((planes, rows, lanes), F32)
    return tuple(
        call(
            lambda *refs: final_kernel(cells, *refs), "final",
            [shifts, lines, *basis, *images], [SM] + [VM] * 10,
            [jax.ShapeDtypeStruct((5, planes, rows, lanes), F32), jax.ShapeDtypeStruct((5, 5), F32), whole, whole],
            out_specs=[ANY, VM, ANY, ANY],
            scratch=[pltpu.VMEM((7, planes, rows, lanes), F32), pltpu.SemaphoreType.DMA((planes, 3))],
        )
    )


def solution(mesh):
    torus = Mesh(mesh.devices.reshape(4, 8, 2, mesh.shape["gy"]), EVERY)
    in_specs = (P(GX, "gy", None), P(None, GX, "gy", None), P())
    out_specs = (P(None, GX, "gy", None), P(), P(GX, "gy", None), P(GX, "gy", None))
    return jax.shard_map(body, mesh=torus, in_specs=in_specs, out_specs=out_specs, check_vma=False)
```

```python
import functools

import jax
import jax.numpy as jnp
from jax import lax
from jax.experimental import pallas as pl
from jax.experimental.pallas import tpu as pltpu
from jax.sharding import Mesh
from jax.sharding import PartitionSpec as P

GX = ("gx_0", "gx_1", "gx_2")
EVERY = ("gx_0", "gx_1", "gx_2", "gy")
F32 = jnp.float32
GROWTH = 2.0
LIMIT = 8 * 1024 * 1024

VM = pl.BlockSpec(memory_space=pltpu.VMEM)
SM = pl.BlockSpec(memory_space=pltpu.SMEM)
ANY = pl.BlockSpec(memory_space=pl.ANY)


def on_chip(*shape):
    return pltpu.VMEM(shape, F32)


def pinned(array):
    return pltpu.with_memory_space_constraint(array, pltpu.VMEM)


def in_hbm(array):
    return pltpu.with_memory_space_constraint(array, pltpu.HBM)


def call(kernel, name, ins, specs, outs, out_specs=None, scratch=(), aliases=None):
    ins = [pinned(a) if s is VM else in_hbm(a) if s is ANY else a for a, s in zip(ins, specs)]
    return pl.pallas_call(
        kernel,
        name=name,
        out_shape=outs,
        in_specs=specs,
        out_specs=out_specs if out_specs is not None else [VM] * len(outs),
        scratch_shapes=scratch,
        input_output_aliases=aliases or {},
        compiler_params=pltpu.CompilerParams(vmem_limit_bytes=LIMIT),
    )(*ins)


G = 8


def run_copies(pairs, sems):
    copies = [pltpu.make_async_copy(s, t, sems.at[n]) for n, (s, t) in enumerate(pairs)]
    for copy in copies:
        copy.start()
    for copy in copies:
        copy.wait()


EARLY = 4


def cut_rows_kernel(rhs, coefs, y_low, y_high, sems):
    planes, rows = rhs.shape[0], rhs.shape[1]
    pairs = []
    for y, span in ((y_low, slice(0, G)), (y_high, slice(rows - G, rows))):
        pairs.append((rhs.at[:, span], y.at[0:planes]))
        pairs.append((coefs.at[0:7, 0, span], y.at[planes : planes + 7]))
        pairs.append((coefs.at[0:7, planes - 1, span], y.at[planes + 7 : planes + 14]))
        for d in range(EARLY):
            at = planes + 14 + (planes - 2) * d
            pairs.append((coefs.at[d, 1 : planes - 1, span], y.at[at : at + planes - 2]))
    run_copies(pairs, sems)


def cut_rest_kernel(coefs, after, y_low, y_high, sems):
    planes, rows = coefs.shape[1], coefs.shape[2]
    pairs = []
    inner = planes - 2
    for y, span in ((y_low, slice(0, G)), (y_high, slice(rows - G, rows))):
        for d in range(EARLY, 7):
            at = inner * (d - EARLY)
            pairs.append((coefs.at[d, 1 : planes - 1, span], y.at[at : at + inner]))
        for d in range(6):
            at = (7 - EARLY) * inner + planes * d
            pairs.append((coefs.at[7 + d, :, span], y.at[at : at + planes]))
    run_copies(pairs, sems)


def load_kernel(rhs, coefs, after, field, own, sems):
    planes, rows = rhs.shape[0], rhs.shape[1]
    pairs = [(rhs, field.at[:, G : rows + G])]
    for p in range(planes):
        pairs.append((coefs.at[:, p], own.at[:, rows * p : rows * p + rows]))
    run_copies(pairs, sems)


def tile_at(row):
    return pl.ds(pl.multiple_of(row, 8), 8)


def ghosted(t, tiles, below, middle, above):
    if t == 0:
        return below()
    if t == tiles - 1:
        return above()
    return middle(8 * t - 8)


def edges():
    place = lax.axis_index("gy")
    last = lax.axis_size("gy") - 1
    return jnp.where(place > 0, 1.0, 0.0), jnp.where(place < last, 1.0, 0.0)


def within(edge, t, tiles, value):
    if t == 0:
        return value * edge[0]
    if t == tiles - 1:
        return value * edge[1]
    return value


def stencil(field, at, emit, skip=None, only=None):
    tiles = field.shape[1] // 8
    lanes = field.shape[2]
    row = lax.broadcasted_iota(jnp.int32, (8, lanes), 0)
    lane = lax.broadcasted_iota(jnp.int32, (8, lanes), 1)
    top, bottom = row == 0, row == 7
    left, right = lane == 0, lane == lanes - 1

    def tile(t):
        value = field[at, 8 * t : 8 * t + 8, :]
        return value, pltpu.roll(value, 1, 0), pltpu.roll(value, 7, 0)

    if only == "ghosts":
        ends = tile(tiles - 2), tile(tiles - 1)
    before = here = tile(0)
    for t in range(tiles):
        if only == "ghosts" and 0 < t < tiles - 1:
            before, here = ends
            continue
        after = tile(t + 1) if t + 1 < tiles else here
        value = here[0]
        span = slice(8 * t, 8 * t + 8)
        near = [
            None if skip == 0 else field[at - 1, span, :],
            None if skip == 1 else field[at + 1, span, :],
            jnp.where(top, before[1], here[1]),
            jnp.where(bottom, after[2], here[2]),
            jnp.where(left, 0.0, pltpu.roll(value, 1, 1)),
            jnp.where(right, 0.0, pltpu.roll(value, lanes - 1, 1)),
        ]
        if only != "own" or 0 < t < tiles - 1:
            emit(t, span, value, near)
        before, here = here, after


def spai_plane(edge, coefficient, field, at, store, skip=None, only=None):
    tiles = field.shape[1] // 8

    def emit(t, span, value, near):
        total = coefficient(0, t) * value
        for d in range(6):
            if near[d] is not None:
                total = total + coefficient(1 + d, t) * near[d]
        store(span, within(edge, t, tiles, total))

    stencil(field, at, emit, skip, only)


def face_coefficient(side, planes, tiles, middle, y_below, y_above):
    at = planes + 7 * side
    return lambda d, t: ghosted(t, tiles, lambda: y_below[at + d], lambda r: middle(d, r), lambda: y_above[at + d])


def face_kernel(field, own, y_below, y_above, x_low, x_high, hold):
    edge = edges()
    planes, tall = field.shape[0], field.shape[1]
    rows, tiles = tall - 2 * G, tall // 8
    for n, p in enumerate((0, 1, planes - 2, planes - 1)):
        hold[n, 0:G, :] = y_below[p] * edge[0]
        hold[n, G : tall - G, :] = field[p, G : tall - G, :]
        hold[n, tall - G : tall, :] = y_above[p] * edge[1]
    for side, (x, at, p) in enumerate(((x_low, 0, 0), (x_high, 3, planes - 1))):
        coefficient = face_coefficient(
            side, planes, tiles, lambda d, r: own[d, rows * p + r : rows * p + r + 8, :], y_below, y_above
        )

        def store(span, value):
            x[0, span, :] = value

        spai_plane(edge, coefficient, hold, at, store, skip=side)
        x[1] = hold[at]
        for t in range(tiles):
            x[2, 8 * t : 8 * t + 8, :] = coefficient(1 + side, t)


def oper_coefficient(planes, rows, tiles, own, z_below, z_above, p):
    def coefficient(d, t):
        at = (7 - EARLY) * (planes - 2) + planes * d + p
        return ghosted(
            t, tiles, lambda: z_below[at], lambda r: own[7 + d, tile_at(rows * p + r), :], lambda: z_above[at]
        )

    return coefficient


def oper_plane(edge, shift, own, z_below, z_above, field, image, out, p, skip=None):
    planes, tiles = field.shape[0], field.shape[1] // 8
    rows = field.shape[1] - 2 * G

    coefficient = oper_coefficient(planes, rows, tiles, own, z_below, z_above, p)

    def emit(t, span, value, near):
        total = value - shift * field[p, span, :]
        for d in range(6):
            if near[d] is not None:
                total = total - coefficient(d, t) * near[d]
        out[p, span, :] = within(edge, t, tiles, GROWTH * total)

    stencil(image, p + 1, emit, skip)


def each(first, count, jump, work):
    half = count // 2

    def one(n, carry):
        work(first + n + jump * (n // half))
        return carry

    lax.fori_loop(0, count, one, 0)


def image_planes(edge, own, z_below, z_above, y_below, y_above, field, image, only=None):
    planes, tiles = field.shape[0], field.shape[1] // 8
    rows = field.shape[1] - 2 * G

    def image_plane(p):
        def coefficient(d, t):
            if only == "own":
                return own[d, tile_at(rows * p + 8 * t - 8), :]
            ghosts = (y_below, y_above) if d < EARLY else (z_below, z_above)
            at = planes + 14 + (planes - 2) * d if d < EARLY else (planes - 2) * (d - EARLY)
            below, above = (ghost.at[at + p - 1] for ghost in ghosts)
            return ghosted(t, tiles, lambda: below[...], lambda r: own[d, tile_at(rows * p + r), :], lambda: above[...])

        def store(span, value):
            image[p + 1, span, :] = value

        spai_plane(edge, coefficient, field, p, store, None, only)

    each(1, planes - 2, 0, image_plane)


def inner_work(shift, edge, own, z_below, z_above, y_below, y_above, field, image, out, only=None):
    planes = field.shape[0]
    image_planes(edge, own, z_below, z_above, y_below, y_above, field, image, only)
    each(2, planes - 4, 0, lambda p: oper_plane(edge, shift, own, z_below, z_above, field, image, out, p))
    for skip, p in ((0, 1), (1, planes - 2)):
        oper_plane(edge, shift, own, z_below, z_above, field, image, out, p, skip)


def first_own_kernel(own, y_below, y_above, field0, field, image):
    edge = edges()
    planes, tall = field.shape[0], field.shape[1]
    field[:, 0:G, :] = y_below[0:planes] * edge[0]
    field[:, tall - G : tall, :] = y_above[0:planes] * edge[1]
    image_planes(edge, own, None, None, y_below, y_above, field, image, "own")


def first_inner_kernel(shifts, own, z_below, z_above, y_below, y_above, field, image0, image, out):
    inner_work(shifts[0], edges(), own, z_below, z_above, y_below, y_above, field, image, out, "ghosts")


def inner_kernel(step, shifts, own, z_below, z_above, y_below, y_above, field, image, out):
    inner_work(shifts[step], edges(), own, z_below, z_above, y_below, y_above, field, image, out)


def outer_kernel(step, shifts, own, z_below, z_above, y_below, y_above, far_low, far_high, my_low, my_high, *refs):
    if step == 0:
        low, high, below, above = my_low, my_high, far_low, far_high
    else:
        low, high, below, above, *refs = refs
    if step == 3:
        refs = refs[1:]
    field, image0, out0, image, out, *sends = refs
    edge = edges()
    planes, tall = field.shape[0], field.shape[1]
    rows, tiles = tall - 2 * G, tall // 8
    for t in range(tiles):
        span = slice(8 * t, 8 * t + 8)
        image[0, span, :] = below[0, span, :] + far_low[2, span, :] * field[0, span, :]
        image[1, span, :] = low[0, span, :] + my_low[2, span, :] * below[1, span, :]
        image[planes, span, :] = high[0, span, :] + my_high[2, span, :] * above[1, span, :]
        image[planes + 1, span, :] = above[0, span, :] + far_high[2, span, :] * field[planes - 1, span, :]
    for skip, p, face in ((0, 1, 1), (1, planes - 2, planes)):
        coefficient = oper_coefficient(planes, rows, tiles, own, z_below, z_above, p)
        for t in range(tiles):
            span = slice(8 * t, 8 * t + 8)
            out[p, span, :] = out[p, span, :] - GROWTH * (coefficient(skip, t) * image[face, span, :])
    each(0, 2, planes - 2, lambda p: oper_plane(edge, shifts[step], own, z_below, z_above, field, image, out, p))
    for side, (x, at) in enumerate(zip(sends, (0, planes - 1))):
        coefficient = face_coefficient(
            side, planes, tiles, lambda d, r: own[d, rows * at + r : rows * at + r + 8, :], y_below, y_above
        )

        def store(span, value):
            x[0, span, :] = value

        spai_plane(edge, coefficient, out, at, store, skip=side)
        x[1] = out[at]


def pair_rows(count):
    return [(i, j) for j in range(count) for i in range(j + 1)]


def gram_rows(fields, pairs, out, start):
    planes = fields[0].shape[0]
    rows = fields[0].shape[1] - 2 * G

    def one(p, sums):
        sums = list(sums)
        for r in range(G, rows + G, 8):
            values = [f[p, r : r + 8, :] for f in fields]
            for k, (i, j) in enumerate(pairs):
                sums[k] = sums[k] + values[i] * values[j]
        return tuple(sums)

    zero = jnp.zeros((8, fields[0].shape[2]), F32)
    sums = lax.fori_loop(0, planes, one, tuple(zero for _ in pairs))
    for k, s in enumerate(sums):
        out[start + k : start + k + 1, :] = jnp.sum(s[:, :128] + s[:, 128:], axis=0, keepdims=True)


def early_gram_kernel(v0, v1, v2, v3, out):
    out[...] = jnp.zeros_like(out)
    gram_rows((v0, v1, v2, v3), pair_rows(4), out, 0)


def late_gram_kernel(early, v0, v1, v2, v3, v4, out, hold):
    hold[...] = early[...]
    gram_rows((v0, v1, v2, v3, v4), [(i, 4) for i in range(5)], hold, 10)
    totals = jnp.sum(hold[...], axis=1, keepdims=True)
    row = lax.broadcasted_iota(jnp.int32, (16, 128), 0)
    lane = lax.broadcasted_iota(jnp.int32, (16, 128), 1)
    line = jnp.sum(jnp.where(row == lane, totals, 0.0), axis=0, keepdims=True)
    out[...] = jnp.broadcast_to(line, out.shape)


def solve(gram, shifts):
    n = 5
    zero = jnp.zeros_like(gram[0][0])
    one = jnp.ones_like(zero)
    lower = [[zero] * n for _ in range(n)]
    for j in range(n):
        rest = gram[j][j]
        for k in range(j):
            rest = rest - lower[j][k] * lower[j][k]
        pivot = jnp.sqrt(rest)
        lower[j][j] = pivot
        for i in range(j + 1, n):
            rest = gram[i][j]
            for k in range(j):
                rest = rest - lower[i][k] * lower[j][k]
            lower[i][j] = rest / pivot
    factor = [[lower[j][i] for j in range(n)] for i in range(n)]

    def invert(upper, order):
        result = [[zero] * order for _ in range(order)]
        for row in range(order - 1, -1, -1):
            for column in range(row, order):
                known = one if column == row else zero
                for k in range(row + 1, column + 1):
                    known = known - upper[row][k] * result[k][column]
                result[row][column] = known / upper[row][row]
        return result

    inverse = invert(factor, n)
    count = n - 1
    hess = [[None] * count for _ in range(n)]
    for row in range(n):
        for column in range(count):
            entry = zero
            if column >= row:
                entry = entry + factor[row][column] * shifts[column]
            if column + 1 >= row:
                entry = entry + factor[row][column + 1] * (1.0 / GROWTH)
            hess[row][column] = entry
    target = [factor[0][0]] + [zero] * (n - 1)
    for column in range(count):
        top, below = hess[column], hess[column + 1]
        radius = jnp.sqrt(top[column] * top[column] + below[column] * below[column])
        cosine = top[column] / radius
        sine = below[column] / radius
        hess[column] = [cosine * t + sine * b for t, b in zip(top, below)]
        hess[column + 1] = [cosine * b - sine * t for t, b in zip(top, below)]
        first, second = target[column], target[column + 1]
        target[column] = cosine * first + sine * second
        target[column + 1] = cosine * second - sine * first
    upper_inverse = invert(hess, count)
    weights = []
    for row in range(count):
        entry = zero
        for k in range(row, count):
            entry = entry + upper_inverse[row][k] * target[k]
        weights.append(entry)
    combine = []
    for row in range(n):
        entry = one if row == 0 else zero
        if row < count:
            entry = entry - shifts[row] * weights[row]
        if row > 0:
            entry = entry - (1.0 / GROWTH) * weights[row - 1]
        combine.append(entry)
    return factor, inverse, weights, combine


def final_kernel(cells, shifts, rows, v0, v1, v2, v3, v4, w0, w1, w2, w3,
                 basis, factor_out, solution_out, residual_out, made, sems):
    line = jnp.sum(rows[...], axis=0, keepdims=True) * (1.0 / cells)
    gram = [[None] * 5 for _ in range(5)]
    for k, (i, j) in enumerate(pair_rows(5)):
        entry = jnp.broadcast_to(line[:, k : k + 1], (8, 128))
        gram[i][j] = entry
        gram[j][i] = entry
    factor, inverse, weights, combine = solve(gram, [shifts[k] for k in range(4)])
    row = lax.broadcasted_iota(jnp.int32, (8, 128), 0)
    lane = lax.broadcasted_iota(jnp.int32, (8, 128), 1)
    table = jnp.zeros((8, 128), F32)
    for i in range(5):
        for j in range(i, 5):
            table = jnp.where((row == i) & (lane == j), factor[i][j], table)
    factor_out[...] = table[:5, :5]
    fields = (v0, v1, v2, v3, v4)
    images = (w0, w1, w2, w3)
    planes = made.shape[1]

    def copies(p):
        triples = ((made.at[0:5, p], basis.at[:, p]), (made.at[5, p], solution_out.at[p]), (made.at[6, p], residual_out.at[p]))
        return [pltpu.make_async_copy(source, target, sems.at[p, n]) for n, (source, target) in enumerate(triples)]

    def blocks():
        return [(r, c) for r in range(0, made.shape[2], 8) for c in range(0, made.shape[3], 128)]

    def one(p, carry):
        for r, c in blocks():
            v = [f[p, r + G : r + G + 8, c : c + 128] for f in fields]
            for k in range(5):
                total = inverse[0][k] * v[0]
                for j in range(1, k + 1):
                    total = total + inverse[j][k] * v[j]
                made[k, p, r : r + 8, c : c + 128] = total
        first, *others = copies(p)
        first.start()
        for r, c in blocks():
            total = weights[0] * images[0][p + 1, r + G : r + G + 8, c : c + 128]
            for k in range(1, 4):
                total = total + weights[k] * images[k][p + 1, r + G : r + G + 8, c : c + 128]
            made[5, p, r : r + 8, c : c + 128] = total
            total = combine[0] * fields[0][p, r + G : r + G + 8, c : c + 128]
            for j in range(1, 5):
                total = total + combine[j] * fields[j][p, r + G : r + G + 8, c : c + 128]
            made[6, p, r : r + 8, c : c + 128] = total
        for copy in others:
            copy.start()
        return carry

    def finish(p, carry):
        for copy in copies(p):
            copy.wait()
        return carry

    lax.fori_loop(0, planes, one, 0)
    lax.fori_loop(0, planes, finish, 0)


def ring(count, step):
    return [(i, (i + step) % count) for i in range(count)]


def both_ways(low, high, axis):
    count = lax.axis_size(axis)
    return lax.ppermute(high, axis, ring(count, 1)), lax.ppermute(low, axis, ring(count, -1))


def body(rhs, coefs, shifts):
    planes, rows, lanes = rhs.shape
    tall = rows + 2 * G
    field = on_chip(planes, tall, lanes)
    image = on_chip(planes + 2, tall, lanes)
    first_face, face = on_chip(3, tall, lanes), on_chip(2, tall, lanes)
    y_cut = on_chip(planes + 14 + EARLY * (planes - 2), G, lanes)
    z_cut = on_chip((7 - EARLY) * (planes - 2) + 6 * planes, G, lanes)
    y_low, y_high = call(
        cut_rows_kernel, "cut_rows", [rhs, coefs], [ANY] * 2, [y_cut, y_cut], scratch=[pltpu.SemaphoreType.DMA((6 + 2 * EARLY,))]
    )
    y_below, y_above = both_ways(y_low, y_high, "gy")
    z_low, z_high = call(
        cut_rest_kernel, "cut_rest", [coefs, y_low], [ANY, VM], [z_cut, z_cut],
        scratch=[pltpu.SemaphoreType.DMA((2 * (13 - EARLY),))],
    )
    z_below, z_above = both_ways(z_low, z_high, "gy")
    v, own = call(
        load_kernel, "load", [rhs, coefs, z_low], [ANY, ANY, VM], [field, on_chip(13, planes * rows, lanes)],
        scratch=[pltpu.SemaphoreType.DMA((1 + planes,))],
    )
    my_low, my_high = call(
        face_kernel, "face", [v, own, y_below, y_above], [VM] * 4, [first_face, first_face],
        scratch=[pltpu.VMEM((4, tall, lanes), F32)],
    )
    far_low, far_high = both_ways(my_low, my_high, GX)
    basis, images = [], []
    low = high = below = above = None
    for step in range(4):
        common = [shifts, own, z_below, z_above]
        if step == 0:
            v, w = call(
                first_own_kernel, "first_own", [own, y_below, y_above, v], [VM] * 4, [field, image], aliases={3: 0}
            )
            w, out = call(
                first_inner_kernel, "first_inner", common + [y_below, y_above, v, w], [SM] + [VM] * 7,
                [image, field], aliases={7: 0},
            )
        else:
            w, out = call(
                functools.partial(inner_kernel, step), "inner", common + [y_below, y_above, v], [SM] + [VM] * 6, [image, field]
            )
        common += [y_below, y_above, far_low, far_high, my_low, my_high]
        if step > 0:
            common += [low, high, below, above]
        if step == 3:
            (early,) = call(early_gram_kernel, "early_gram", basis + [v], [VM] * 4, [on_chip(16, 128)])
            common += [early]
        common += [v]
        at = len(common)
        w, out, *sends = call(
            functools.partial(outer_kernel, step), "first_outer" if step == 0 else "outer",
            common + [w, out], [SM] + [VM] * (at + 1), [image, field] + [face, face] * (step < 3),
            aliases={at: 0, at + 1: 1},
        )
        if sends:
            low, high = sends
            below, above = both_ways(low, high, GX)
        basis.append(v)
        images.append(w)
        v = out
    basis.append(v)
    devices = lax.axis_size(GX) * lax.axis_size("gy")
    (line,) = call(
        late_gram_kernel, "late_gram", [early, *basis], [VM] * 6, [on_chip(devices, 128)],
        scratch=[pltpu.VMEM((16, 128), F32)],
    )
    lines = lax.all_to_all(line, EVERY, 0, 0, tiled=True)
    cells = float(planes * rows * lanes * devices)
    whole = jax.ShapeDtypeStruct((planes, rows, lanes), F32)
    return tuple(
        call(
            lambda *refs: final_kernel(cells, *refs), "final",
            [shifts, lines, *basis, *images], [SM] + [VM] * 10,
            [jax.ShapeDtypeStruct((5, planes, rows, lanes), F32), jax.ShapeDtypeStruct((5, 5), F32), whole, whole],
            out_specs=[ANY, VM, ANY, ANY],
            scratch=[pltpu.VMEM((7, planes, rows, lanes), F32), pltpu.SemaphoreType.DMA((planes, 3))],
        )
    )


def solution(mesh):
    torus = Mesh(mesh.devices.reshape(4, 8, 2, mesh.shape["gy"]), EVERY)
    in_specs = (P(GX, "gy", None), P(None, GX, "gy", None), P())
    out_specs = (P(None, GX, "gy", None), P(), P(GX, "gy", None), P(GX, "gy", None))
    return jax.shard_map(body, mesh=torus, in_specs=in_specs, out_specs=out_specs, check_vma=False)
```

```python
import functools

import jax
import jax.numpy as jnp
from jax import lax
from jax.experimental import pallas as pl
from jax.experimental.pallas import tpu as pltpu
from jax.sharding import Mesh
from jax.sharding import PartitionSpec as P

GX = ("gx_0", "gx_1", "gx_2")
EVERY = ("gx_0", "gx_1", "gx_2", "gy")
F32 = jnp.float32
GROWTH = 2.0
LIMIT = 8 * 1024 * 1024

VM = pl.BlockSpec(memory_space=pltpu.VMEM)
SM = pl.BlockSpec(memory_space=pltpu.SMEM)
ANY = pl.BlockSpec(memory_space=pl.ANY)


def on_chip(*shape):
    return pltpu.VMEM(shape, F32)


def pinned(array):
    return pltpu.with_memory_space_constraint(array, pltpu.VMEM)


def in_hbm(array):
    return pltpu.with_memory_space_constraint(array, pltpu.HBM)


def call(kernel, name, ins, specs, outs, out_specs=None, scratch=(), aliases=None):
    ins = [pinned(a) if s is VM else in_hbm(a) if s is ANY else a for a, s in zip(ins, specs)]
    return pl.pallas_call(
        kernel,
        name=name,
        out_shape=outs,
        in_specs=specs,
        out_specs=out_specs if out_specs is not None else [VM] * len(outs),
        scratch_shapes=scratch,
        input_output_aliases=aliases or {},
        compiler_params=pltpu.CompilerParams(vmem_limit_bytes=LIMIT),
    )(*ins)


G = 8


def run_copies(pairs, sems):
    copies = [pltpu.make_async_copy(s, t, sems.at[n]) for n, (s, t) in enumerate(pairs)]
    for copy in copies:
        copy.start()
    for copy in copies:
        copy.wait()


EARLY = 6


def cut_rows_kernel(rhs, coefs, y_low, y_high, sems):
    planes, rows = rhs.shape[0], rhs.shape[1]
    pairs = []
    for y, span in ((y_low, slice(0, G)), (y_high, slice(rows - G, rows))):
        pairs.append((rhs.at[:, span], y.at[0:planes]))
        pairs.append((coefs.at[0:7, 0, span], y.at[planes : planes + 7]))
        pairs.append((coefs.at[0:7, planes - 1, span], y.at[planes + 7 : planes + 14]))
        for d in range(EARLY):
            at = planes + 14 + (planes - 2) * d
            pairs.append((coefs.at[d, 1 : planes - 1, span], y.at[at : at + planes - 2]))
    run_copies(pairs, sems)


def cut_rest_kernel(coefs, after, y_low, y_high, sems):
    planes, rows = coefs.shape[1], coefs.shape[2]
    pairs = []
    inner = planes - 2
    for y, span in ((y_low, slice(0, G)), (y_high, slice(rows - G, rows))):
        for d in range(EARLY, 7):
            at = inner * (d - EARLY)
            pairs.append((coefs.at[d, 1 : planes - 1, span], y.at[at : at + inner]))
        for d in range(6):
            at = (7 - EARLY) * inner + planes * d
            pairs.append((coefs.at[7 + d, :, span], y.at[at : at + planes]))
    run_copies(pairs, sems)


def load_kernel(rhs, coefs, after, field, own, sems):
    planes, rows = rhs.shape[0], rhs.shape[1]
    pairs = [(rhs, field.at[:, G : rows + G])]
    for p in range(planes):
        pairs.append((coefs.at[:, p], own.at[:, rows * p : rows * p + rows]))
    run_copies(pairs, sems)


def tile_at(row):
    return pl.ds(pl.multiple_of(row, 8), 8)


def ghosted(t, tiles, below, middle, above):
    if t == 0:
        return below()
    if t == tiles - 1:
        return above()
    return middle(8 * t - 8)


def edges():
    place = lax.axis_index("gy")
    last = lax.axis_size("gy") - 1
    return jnp.where(place > 0, 1.0, 0.0), jnp.where(place < last, 1.0, 0.0)


def within(edge, t, tiles, value):
    if t == 0:
        return value * edge[0]
    if t == tiles - 1:
        return value * edge[1]
    return value


def stencil(field, at, emit, skip=None, only=None):
    tiles = field.shape[1] // 8
    lanes = field.shape[2]
    row = lax.broadcasted_iota(jnp.int32, (8, lanes), 0)
    lane = lax.broadcasted_iota(jnp.int32, (8, lanes), 1)
    top, bottom = row == 0, row == 7
    left, right = lane == 0, lane == lanes - 1

    def tile(t):
        value = field[at, 8 * t : 8 * t + 8, :]
        return value, pltpu.roll(value, 1, 0), pltpu.roll(value, 7, 0)

    if only == "ghosts":
        ends = tile(tiles - 2), tile(tiles - 1)
    before = here = tile(0)
    for t in range(tiles):
        if only == "ghosts" and 0 < t < tiles - 1:
            before, here = ends
            continue
        after = tile(t + 1) if t + 1 < tiles else here
        value = here[0]
        span = slice(8 * t, 8 * t + 8)
        near = [
            None if skip == 0 else field[at - 1, span, :],
            None if skip == 1 else field[at + 1, span, :],
            jnp.where(top, before[1], here[1]),
            jnp.where(bottom, after[2], here[2]),
            jnp.where(left, 0.0, pltpu.roll(value, 1, 1)),
            jnp.where(right, 0.0, pltpu.roll(value, lanes - 1, 1)),
        ]
        if only != "own" or 0 < t < tiles - 1:
            emit(t, span, value, near)
        before, here = here, after


def spai_plane(edge, coefficient, field, at, store, skip=None, only=None):
    tiles = field.shape[1] // 8

    def emit(t, span, value, near):
        total = coefficient(0, t) * value
        for d in range(6):
            if near[d] is not None:
                total = total + coefficient(1 + d, t) * near[d]
        store(span, within(edge, t, tiles, total))

    stencil(field, at, emit, skip, only)


def face_coefficient(side, planes, tiles, middle, y_below, y_above):
    at = planes + 7 * side
    return lambda d, t: ghosted(t, tiles, lambda: y_below[at + d], lambda r: middle(d, r), lambda: y_above[at + d])


def face_kernel(field, own, y_below, y_above, x_low, x_high, hold):
    edge = edges()
    planes, tall = field.shape[0], field.shape[1]
    rows, tiles = tall - 2 * G, tall // 8
    for n, p in enumerate((0, 1, planes - 2, planes - 1)):
        hold[n, 0:G, :] = y_below[p] * edge[0]
        hold[n, G : tall - G, :] = field[p, G : tall - G, :]
        hold[n, tall - G : tall, :] = y_above[p] * edge[1]
    for side, (x, at, p) in enumerate(((x_low, 0, 0), (x_high, 3, planes - 1))):
        coefficient = face_coefficient(
            side, planes, tiles, lambda d, r: own[d, rows * p + r : rows * p + r + 8, :], y_below, y_above
        )

        def store(span, value):
            x[0, span, :] = value

        spai_plane(edge, coefficient, hold, at, store, skip=side)
        x[1] = hold[at]
        for t in range(tiles):
            x[2, 8 * t : 8 * t + 8, :] = coefficient(1 + side, t)


def oper_coefficient(planes, rows, tiles, own, z_below, z_above, p):
    def coefficient(d, t):
        at = (7 - EARLY) * (planes - 2) + planes * d + p
        return ghosted(
            t, tiles, lambda: z_below[at], lambda r: own[7 + d, tile_at(rows * p + r), :], lambda: z_above[at]
        )

    return coefficient


def oper_plane(edge, shift, own, z_below, z_above, field, image, out, p, skip=None):
    planes, tiles = field.shape[0], field.shape[1] // 8
    rows = field.shape[1] - 2 * G

    coefficient = oper_coefficient(planes, rows, tiles, own, z_below, z_above, p)

    def emit(t, span, value, near):
        total = value - shift * field[p, span, :]
        for d in range(6):
            if near[d] is not None:
                total = total - coefficient(d, t) * near[d]
        out[p, span, :] = within(edge, t, tiles, GROWTH * total)

    stencil(image, p + 1, emit, skip)


def each(first, count, jump, work):
    half = count // 2

    def one(n, carry):
        work(first + n + jump * (n // half))
        return carry

    lax.fori_loop(0, count, one, 0)


def image_planes(edge, own, z_below, z_above, y_below, y_above, field, image, only=None):
    planes, tiles = field.shape[0], field.shape[1] // 8
    rows = field.shape[1] - 2 * G

    def image_plane(p):
        def coefficient(d, t):
            if only == "own":
                return own[d, tile_at(rows * p + 8 * t - 8), :]
            ghosts = (y_below, y_above) if d < EARLY else (z_below, z_above)
            at = planes + 14 + (planes - 2) * d if d < EARLY else (planes - 2) * (d - EARLY)
            below, above = (ghost.at[at + p - 1] for ghost in ghosts)
            return ghosted(t, tiles, lambda: below[...], lambda r: own[d, tile_at(rows * p + r), :], lambda: above[...])

        def store(span, value):
            image[p + 1, span, :] = value

        spai_plane(edge, coefficient, field, p, store, None, only)

    each(1, planes - 2, 0, image_plane)


def inner_work(shift, edge, own, z_below, z_above, y_below, y_above, field, image, out, only=None):
    planes = field.shape[0]
    image_planes(edge, own, z_below, z_above, y_below, y_above, field, image, only)
    each(2, planes - 4, 0, lambda p: oper_plane(edge, shift, own, z_below, z_above, field, image, out, p))
    for skip, p in ((0, 1), (1, planes - 2)):
        oper_plane(edge, shift, own, z_below, z_above, field, image, out, p, skip)


def first_own_kernel(own, y_below, y_above, field0, field, image):
    edge = edges()
    planes, tall = field.shape[0], field.shape[1]
    field[:, 0:G, :] = y_below[0:planes] * edge[0]
    field[:, tall - G : tall, :] = y_above[0:planes] * edge[1]
    image_planes(edge, own, None, None, y_below, y_above, field, image, "own")


def first_inner_kernel(shifts, own, z_below, z_above, y_below, y_above, field, image0, image, out):
    inner_work(shifts[0], edges(), own, z_below, z_above, y_below, y_above, field, image, out, "ghosts")


def inner_kernel(step, shifts, own, z_below, z_above, y_below, y_above, field, image, out):
    inner_work(shifts[step], edges(), own, z_below, z_above, y_below, y_above, field, image, out)


def outer_kernel(step, shifts, own, z_below, z_above, y_below, y_above, far_low, far_high, my_low, my_high, *refs):
    if step == 0:
        low, high, below, above = my_low, my_high, far_low, far_high
    else:
        low, high, below, above, *refs = refs
    if step == 3:
        refs = refs[1:]
    field, image0, out0, image, out, *sends = refs
    edge = edges()
    planes, tall = field.shape[0], field.shape[1]
    rows, tiles = tall - 2 * G, tall // 8
    for t in range(tiles):
        span = slice(8 * t, 8 * t + 8)
        image[0, span, :] = below[0, span, :] + far_low[2, span, :] * field[0, span, :]
        image[1, span, :] = low[0, span, :] + my_low[2, span, :] * below[1, span, :]
        image[planes, span, :] = high[0, span, :] + my_high[2, span, :] * above[1, span, :]
        image[planes + 1, span, :] = above[0, span, :] + far_high[2, span, :] * field[planes - 1, span, :]
    for skip, p, face in ((0, 1, 1), (1, planes - 2, planes)):
        coefficient = oper_coefficient(planes, rows, tiles, own, z_below, z_above, p)
        for t in range(tiles):
            span = slice(8 * t, 8 * t + 8)
            out[p, span, :] = out[p, span, :] - GROWTH * (coefficient(skip, t) * image[face, span, :])
    each(0, 2, planes - 2, lambda p: oper_plane(edge, shifts[step], own, z_below, z_above, field, image, out, p))
    for side, (x, at) in enumerate(zip(sends, (0, planes - 1))):
        coefficient = face_coefficient(
            side, planes, tiles, lambda d, r: own[d, rows * at + r : rows * at + r + 8, :], y_below, y_above
        )

        def store(span, value):
            x[0, span, :] = value

        spai_plane(edge, coefficient, out, at, store, skip=side)
        x[1] = out[at]


def pair_rows(count):
    return [(i, j) for j in range(count) for i in range(j + 1)]


def gram_rows(fields, pairs, out, start):
    planes = fields[0].shape[0]
    rows = fields[0].shape[1] - 2 * G

    def one(p, sums):
        sums = list(sums)
        for r in range(G, rows + G, 8):
            values = [f[p, r : r + 8, :] for f in fields]
            for k, (i, j) in enumerate(pairs):
                sums[k] = sums[k] + values[i] * values[j]
        return tuple(sums)

    zero = jnp.zeros((8, fields[0].shape[2]), F32)
    sums = lax.fori_loop(0, planes, one, tuple(zero for _ in pairs))
    for k, s in enumerate(sums):
        out[start + k : start + k + 1, :] = jnp.sum(s[:, :128] + s[:, 128:], axis=0, keepdims=True)


def early_gram_kernel(v0, v1, v2, v3, out):
    out[...] = jnp.zeros_like(out)
    gram_rows((v0, v1, v2, v3), pair_rows(4), out, 0)


def late_gram_kernel(early, v0, v1, v2, v3, v4, out, hold):
    hold[...] = early[...]
    gram_rows((v0, v1, v2, v3, v4), [(i, 4) for i in range(5)], hold, 10)
    totals = jnp.sum(hold[...], axis=1, keepdims=True)
    row = lax.broadcasted_iota(jnp.int32, (16, 128), 0)
    lane = lax.broadcasted_iota(jnp.int32, (16, 128), 1)
    line = jnp.sum(jnp.where(row == lane, totals, 0.0), axis=0, keepdims=True)
    out[...] = jnp.broadcast_to(line, out.shape)


def solve(gram, shifts):
    n = 5
    zero = jnp.zeros_like(gram[0][0])
    one = jnp.ones_like(zero)
    lower = [[zero] * n for _ in range(n)]
    for j in range(n):
        rest = gram[j][j]
        for k in range(j):
            rest = rest - lower[j][k] * lower[j][k]
        pivot = jnp.sqrt(rest)
        lower[j][j] = pivot
        for i in range(j + 1, n):
            rest = gram[i][j]
            for k in range(j):
                rest = rest - lower[i][k] * lower[j][k]
            lower[i][j] = rest / pivot
    factor = [[lower[j][i] for j in range(n)] for i in range(n)]

    def invert(upper, order):
        result = [[zero] * order for _ in range(order)]
        for row in range(order - 1, -1, -1):
            for column in range(row, order):
                known = one if column == row else zero
                for k in range(row + 1, column + 1):
                    known = known - upper[row][k] * result[k][column]
                result[row][column] = known / upper[row][row]
        return result

    inverse = invert(factor, n)
    count = n - 1
    hess = [[None] * count for _ in range(n)]
    for row in range(n):
        for column in range(count):
            entry = zero
            if column >= row:
                entry = entry + factor[row][column] * shifts[column]
            if column + 1 >= row:
                entry = entry + factor[row][column + 1] * (1.0 / GROWTH)
            hess[row][column] = entry
    target = [factor[0][0]] + [zero] * (n - 1)
    for column in range(count):
        top, below = hess[column], hess[column + 1]
        radius = jnp.sqrt(top[column] * top[column] + below[column] * below[column])
        cosine = top[column] / radius
        sine = below[column] / radius
        hess[column] = [cosine * t + sine * b for t, b in zip(top, below)]
        hess[column + 1] = [cosine * b - sine * t for t, b in zip(top, below)]
        first, second = target[column], target[column + 1]
        target[column] = cosine * first + sine * second
        target[column + 1] = cosine * second - sine * first
    upper_inverse = invert(hess, count)
    weights = []
    for row in range(count):
        entry = zero
        for k in range(row, count):
            entry = entry + upper_inverse[row][k] * target[k]
        weights.append(entry)
    combine = []
    for row in range(n):
        entry = one if row == 0 else zero
        if row < count:
            entry = entry - shifts[row] * weights[row]
        if row > 0:
            entry = entry - (1.0 / GROWTH) * weights[row - 1]
        combine.append(entry)
    return factor, inverse, weights, combine


def final_kernel(cells, shifts, rows, v0, v1, v2, v3, v4, w0, w1, w2, w3,
                 basis, factor_out, solution_out, residual_out, made, sems):
    line = jnp.sum(rows[...], axis=0, keepdims=True) * (1.0 / cells)
    gram = [[None] * 5 for _ in range(5)]
    for k, (i, j) in enumerate(pair_rows(5)):
        entry = jnp.broadcast_to(line[:, k : k + 1], (8, 128))
        gram[i][j] = entry
        gram[j][i] = entry
    factor, inverse, weights, combine = solve(gram, [shifts[k] for k in range(4)])
    row = lax.broadcasted_iota(jnp.int32, (8, 128), 0)
    lane = lax.broadcasted_iota(jnp.int32, (8, 128), 1)
    table = jnp.zeros((8, 128), F32)
    for i in range(5):
        for j in range(i, 5):
            table = jnp.where((row == i) & (lane == j), factor[i][j], table)
    factor_out[...] = table[:5, :5]
    fields = (v0, v1, v2, v3, v4)
    images = (w0, w1, w2, w3)
    planes = made.shape[1]

    def copies(p):
        triples = ((made.at[0:5, p], basis.at[:, p]), (made.at[5, p], solution_out.at[p]), (made.at[6, p], residual_out.at[p]))
        return [pltpu.make_async_copy(source, target, sems.at[p, n]) for n, (source, target) in enumerate(triples)]

    def blocks():
        return [(r, c) for r in range(0, made.shape[2], 8) for c in range(0, made.shape[3], 128)]

    def one(p, carry):
        for r, c in blocks():
            v = [f[p, r + G : r + G + 8, c : c + 128] for f in fields]
            for k in range(5):
                total = inverse[0][k] * v[0]
                for j in range(1, k + 1):
                    total = total + inverse[j][k] * v[j]
                made[k, p, r : r + 8, c : c + 128] = total
        first, *others = copies(p)
        first.start()
        for r, c in blocks():
            total = weights[0] * images[0][p + 1, r + G : r + G + 8, c : c + 128]
            for k in range(1, 4):
                total = total + weights[k] * images[k][p + 1, r + G : r + G + 8, c : c + 128]
            made[5, p, r : r + 8, c : c + 128] = total
            total = combine[0] * fields[0][p, r + G : r + G + 8, c : c + 128]
            for j in range(1, 5):
                total = total + combine[j] * fields[j][p, r + G : r + G + 8, c : c + 128]
            made[6, p, r : r + 8, c : c + 128] = total
        for copy in others:
            copy.start()
        return carry

    def finish(p, carry):
        for copy in copies(p):
            copy.wait()
        return carry

    lax.fori_loop(0, planes, one, 0)
    lax.fori_loop(0, planes, finish, 0)


def ring(count, step):
    return [(i, (i + step) % count) for i in range(count)]


def both_ways(low, high, axis):
    count = lax.axis_size(axis)
    return lax.ppermute(high, axis, ring(count, 1)), lax.ppermute(low, axis, ring(count, -1))


def body(rhs, coefs, shifts):
    planes, rows, lanes = rhs.shape
    tall = rows + 2 * G
    field = on_chip(planes, tall, lanes)
    image = on_chip(planes + 2, tall, lanes)
    first_face, face = on_chip(3, tall, lanes), on_chip(2, tall, lanes)
    y_cut = on_chip(planes + 14 + EARLY * (planes - 2), G, lanes)
    z_cut = on_chip((7 - EARLY) * (planes - 2) + 6 * planes, G, lanes)
    y_low, y_high = call(
        cut_rows_kernel, "cut_rows", [rhs, coefs], [ANY] * 2, [y_cut, y_cut], scratch=[pltpu.SemaphoreType.DMA((6 + 2 * EARLY,))]
    )
    y_below, y_above = both_ways(y_low, y_high, "gy")
    z_low, z_high = call(
        cut_rest_kernel, "cut_rest", [coefs, y_low], [ANY, VM], [z_cut, z_cut],
        scratch=[pltpu.SemaphoreType.DMA((2 * (13 - EARLY),))],
    )
    z_below, z_above = both_ways(z_low, z_high, "gy")
    v, own = call(
        load_kernel, "load", [rhs, coefs, z_low], [ANY, ANY, VM], [field, on_chip(13, planes * rows, lanes)],
        scratch=[pltpu.SemaphoreType.DMA((1 + planes,))],
    )
    my_low, my_high = call(
        face_kernel, "face", [v, own, y_below, y_above], [VM] * 4, [first_face, first_face],
        scratch=[pltpu.VMEM((4, tall, lanes), F32)],
    )
    far_low, far_high = both_ways(my_low, my_high, GX)
    basis, images = [], []
    low = high = below = above = None
    for step in range(4):
        common = [shifts, own, z_below, z_above]
        if step == 0:
            v, w = call(
                first_own_kernel, "first_own", [own, y_below, y_above, v], [VM] * 4, [field, image], aliases={3: 0}
            )
            w, out = call(
                first_inner_kernel, "first_inner", common + [y_below, y_above, v, w], [SM] + [VM] * 7,
                [image, field], aliases={7: 0},
            )
        else:
            w, out = call(
                functools.partial(inner_kernel, step), "inner", common + [y_below, y_above, v], [SM] + [VM] * 6, [image, field]
            )
        common += [y_below, y_above, far_low, far_high, my_low, my_high]
        if step > 0:
            common += [low, high, below, above]
        if step == 3:
            (early,) = call(early_gram_kernel, "early_gram", basis + [v], [VM] * 4, [on_chip(16, 128)])
            common += [early]
        common += [v]
        at = len(common)
        w, out, *sends = call(
            functools.partial(outer_kernel, step), "first_outer" if step == 0 else "outer",
            common + [w, out], [SM] + [VM] * (at + 1), [image, field] + [face, face] * (step < 3),
            aliases={at: 0, at + 1: 1},
        )
        if sends:
            low, high = sends
            below, above = both_ways(low, high, GX)
        basis.append(v)
        images.append(w)
        v = out
    basis.append(v)
    devices = lax.axis_size(GX) * lax.axis_size("gy")
    (line,) = call(
        late_gram_kernel, "late_gram", [early, *basis], [VM] * 6, [on_chip(devices, 128)],
        scratch=[pltpu.VMEM((16, 128), F32)],
    )
    lines = lax.all_to_all(line, EVERY, 0, 0, tiled=True)
    cells = float(planes * rows * lanes * devices)
    whole = jax.ShapeDtypeStruct((planes, rows, lanes), F32)
    return tuple(
        call(
            lambda *refs: final_kernel(cells, *refs), "final",
            [shifts, lines, *basis, *images], [SM] + [VM] * 10,
            [jax.ShapeDtypeStruct((5, planes, rows, lanes), F32), jax.ShapeDtypeStruct((5, 5), F32), whole, whole],
            out_specs=[ANY, VM, ANY, ANY],
            scratch=[pltpu.VMEM((7, planes, rows, lanes), F32), pltpu.SemaphoreType.DMA((planes, 3))],
        )
    )


def solution(mesh):
    torus = Mesh(mesh.devices.reshape(4, 8, 2, mesh.shape["gy"]), EVERY)
    in_specs = (P(GX, "gy", None), P(None, GX, "gy", None), P())
    out_specs = (P(None, GX, "gy", None), P(), P(GX, "gy", None), P(GX, "gy", None))
    return jax.shard_map(body, mesh=torus, in_specs=in_specs, out_specs=out_specs, check_vma=False)
```
